32 devices in a mesh: seq: 8 (over y, x, core), tp: 4 (over z).
Axes of the slice: x: 2, y: 2, z: 4, core: 2. Of those that a mesh axis runs over, the one named last changes fastest.
Arguments:
- layer_input: bfloat16 [8192, 2048], P('seq', 'tp'), may hold values from -6 to 6
- lengths: int32 [4], replicated, may hold values from 1 to 4096, 8192 in all
- gain_attn: bfloat16 [2048], replicated, may hold values from 0.25 to 1.75
- query_down: bfloat16 [2048, 1024], replicated, may hold values from -0.125 to 0.125
- gain_latent: bfloat16 [1024], replicated, may hold values from 0.25 to 1.75
- query_up: bfloat16 [1024, 4096], P(None, 'tp'), may hold values from -0.1875 to 0.1875
- key_weight: bfloat16 [2048, 256], replicated, may hold values from -0.125 to 0.125
- value_weight: bfloat16 [2048, 256], replicated, may hold values from -0.125 to 0.125
- out_weight: bfloat16 [4096, 2048], P('tp'), may hold values from -0.375 to 0.375
- gain_mlp: bfloat16 [2048], replicated, may hold values from 0.25 to 1.75
- gate_weight: bfloat16 [2048, 5632], P(None, 'tp'), may hold values from -0.125 to 0.125
- up_weight: bfloat16 [2048, 5632], P(None, 'tp'), may hold values from -0.125 to 0.125
- down_weight: bfloat16 [5632, 2048], P('tp'), may hold values from -0.078125 to 0.078125
- cotangent: bfloat16 [8192, 2048], P('seq', 'tp'), may hold values from -6 to 6
Outputs:
- layer_output: float32 [8192, 2048], P('seq', 'tp')
- input_grad: float32 [8192, 2048], P('seq', 'tp')
- gain_attn_grad: float32 [2048], replicated
- query_down_grad: float32 [2048, 1024], P(None, 'tp')
- gain_latent_grad: float32 [1024], replicated
- query_up_grad: float32 [1024, 4096], P(None, 'tp')
- key_weight_grad: float32 [2048, 256], P('tp')
- value_weight_grad: float32 [2048, 256], P('tp')
- out_weight_grad: float32 [4096, 2048], P('tp')
- gain_mlp_grad: float32 [2048], replicated
- gate_weight_grad: float32 [2048, 5632], P(None, 'tp')
- up_weight_grad: float32 [2048, 5632], P(None, 'tp')
- down_weight_grad: float32 [5632, 2048], P('tp')
The draws below stay inside these ranges and needn't reach their ends.
Inputs may be any that keep to these rules, and one draw needn't show every extreme that they name: 4 document lengths that add up to 8192; the longest has exactly 4096 tokens.
All inputs are finite; a program needn't handle non-finite values.
Results may differ from the reference program's by a relative error of at most 0.025.
Values may be sent and summed in bfloat16 or wider, within the bound.
A program may use at most 256 MiB of HBM per device.

```python
import math
import jax
import jax.numpy as jnp
import numpy as np
from jax import lax

D = 2048
HQ = 16
HD = 256
QR = 1024
FF = 5632
NSEQ = 4
KEY_BLOCK = 256
TOKENS = 8192


def shard_levels(rng, dims, pieces, smallest, largest):
    gain, own = 1.0, jax.random.fold_in(rng, 6)
    for axis_at, blocks in pieces:
        draws = jnp.exp(jax.random.uniform(jax.random.fold_in(own, axis_at), (blocks,), jnp.float32, smallest / len(pieces), largest / len(pieces)))
        gain = gain * jnp.repeat(draws, dims[axis_at] // blocks).reshape([-1 if axis == axis_at else 1 for axis in range(len(dims))])
    return gain


def length_profile(amount, total, most, slope):
    loads = [(1 << 20) // math.isqrt(grade ** slope) + 1 for grade in range(2, amount + 1)]
    surplus, counts = total - most - (amount - 1), [1] * (amount - 1)
    while surplus > 0:
        free = [i for i in range(amount - 1) if counts[i] < most]
        pool, remaining = sum([loads[i] for i in free]), surplus
        for i in free:
            more = min(most - counts[i], max(1, remaining * loads[i] // pool), surplus)
            counts[i] = counts[i] + more
            surplus = surplus - more
    return np.array([most] + counts)


def ragged(rng, amount, total, reach, lean):
    if amount == 2:
        one = jax.random.randint(rng, (), max(1, total - reach), min(reach, total - 1) + 1)
        return jnp.stack([one, total - one])
    tallies = jnp.asarray(length_profile(amount, total, reach, lean), jnp.int32)
    couples = (amount - 1) // 2
    donor, receiver = tallies[1:1 + 2 * couples:2], tallies[2:2 + 2 * couples:2]
    slack = jnp.minimum(donor - 1, reach - receiver)
    passed = jax.random.randint(jax.random.fold_in(rng, 1), (couples,), 0, 1 << 20) % (slack + 1)
    tallies = tallies.at[1:1 + 2 * couples:2].set(donor - passed).at[2:2 + 2 * couples:2].set(receiver + passed)
    return tallies[jax.random.permutation(jax.random.fold_in(rng, 2), amount)]


def noise(rng, dims, spread, limit, shards=(), kind=jnp.bfloat16):
    drawn = spread * jax.random.normal(rng, dims, jnp.float32)
    if shards:
        drawn = drawn * shard_levels(rng, dims, shards, -0.22, 0.18)
    return jnp.clip(drawn, -limit, limit).astype(kind)


def setup_inputs(seed: int = 0) -> dict:
    keys = jax.random.split(jax.random.key(seed), 15)
    layer_input = noise(keys[0], (TOKENS, D), 1.0, 6.0, ((0, 8), (1, 4)))
    lengths = ragged(keys[1], NSEQ, TOKENS, TOKENS // 2, 2).astype(jnp.int32)
    gain_attn = jnp.clip(1.0 + 0.15 * jax.random.normal(keys[2], (D,), jnp.float32), 0.25, 1.75).astype(jnp.bfloat16)
    query_down = noise(keys[3], (D, QR), D ** -0.5, 0.125)
    gain_latent = jnp.clip(1.0 + 0.15 * jax.random.normal(keys[4], (QR,), jnp.float32), 0.25, 1.75).astype(jnp.bfloat16)
    query_up = noise(keys[5], (QR, HQ * HD), QR ** -0.5, 0.1875, ((1, 4),))
    key_weight = noise(keys[6], (D, HD), D ** -0.5, 0.125)
    value_weight = noise(keys[7], (D, HD), D ** -0.5, 0.125)
    out_weight = noise(keys[8], (HQ * HD, D), (HQ * HD // 16) ** -0.5, 0.375, ((0, 4),))
    gain_mlp = jnp.clip(1.0 + 0.15 * jax.random.normal(keys[9], (D,), jnp.float32), 0.25, 1.75).astype(jnp.bfloat16)
    gate_weight = noise(keys[10], (D, FF), D ** -0.5, 0.125, ((1, 4),))
    up_weight = noise(keys[11], (D, FF), D ** -0.5, 0.125, ((1, 4),))
    down_weight = noise(keys[12], (FF, D), FF ** -0.5, 0.078125, ((0, 4),))
    cotangent = noise(keys[13], (TOKENS, D), 1.0, 6.0, ((0, 8), (1, 4)))
    return {"layer_input": layer_input, "lengths": lengths, "gain_attn": gain_attn, "query_down": query_down, "gain_latent": gain_latent, "query_up": query_up, "key_weight": key_weight, "value_weight": value_weight, "out_weight": out_weight, "gain_mlp": gain_mlp, "gate_weight": gate_weight, "up_weight": up_weight, "down_weight": down_weight, "cotangent": cotangent}


EPSILON = 1e-05
THETA = 10000.0
MASKED = -1000000000.0

@jax.custom_vjp
def low(v):
    return lax.optimization_barrier(v.astype(jnp.bfloat16)).astype(jnp.float32)

@jax.custom_vjp
def low_back(v):
    return v

def low_keep(v):
    return (low(v), None)

def low_pass(kept, grad):
    return (grad,)

def back_keep(v):
    return (v, None)

def back_low(kept, grad):
    return (low(grad),)
low.defvjp(low_keep, low_pass)
low_back.defvjp(back_keep, back_low)

def matmul(left_op, right_op):
    return jnp.dot(left_op, right_op, precision=lax.Precision.HIGHEST, preferred_element_type=jnp.float32)

def norm_rows(values, gain_vec):
    inverse = lax.rsqrt(lax.optimization_barrier(jnp.mean(values * values, axis=-1, keepdims=True)) + EPSILON)
    return values * inverse * gain_vec

def doc_layout(lengths, token_place):
    doc_ends = jnp.cumsum(lengths).astype(jnp.int32)
    doc_starts = (doc_ends - lengths).astype(jnp.int32)
    segment = lax.optimization_barrier(jnp.sum((doc_ends[None, :] <= token_place[:, None]).astype(jnp.int32), axis=1))
    doc_index = jnp.arange(lengths.shape[0], dtype=jnp.int32)
    doc_start = lax.optimization_barrier(jnp.sum(jnp.where(doc_index[None, :] == segment[:, None], doc_starts[None, :], 0), axis=1)).astype(jnp.int32)
    return (doc_start, (token_place - doc_start).astype(jnp.int32))

def rope_tables(position, head_width):
    half_width = head_width // 2
    frequency = THETA ** (-(jnp.arange(half_width, dtype=jnp.float32) * 2.0 / head_width))
    angles = position.astype(jnp.float32)[:, None] * frequency[None, :]
    return (jnp.cos(angles), jnp.sin(angles))

def rotate(values, cosine, sine):
    half_width = values.shape[-1] // 2
    front_half = values[..., :half_width]
    back_half = values[..., half_width:]
    return jnp.concatenate([front_half * cosine - back_half * sine, front_half * sine + back_half * cosine], axis=-1)

def attend(query_in, key_in, value_in, doc_start):
    blocks = TOKENS // KEY_BLOCK
    key_index = jnp.arange(TOKENS, dtype=jnp.int32)
    score_scale = HD ** (-0.5)

    def one_block(block_args):
        query_blk, start_blk, block_base = block_args
        query_rows = block_base + jnp.arange(KEY_BLOCK, dtype=jnp.int32)
        scores = jnp.einsum('qhd,kd->hqk', query_blk, key_in, precision=lax.Precision.HIGHEST) * score_scale
        scores = low_back(scores)
        allowed = (key_index[None, :] >= start_blk[:, None]) & (key_index[None, :] <= query_rows[:, None])
        scores = jnp.where(allowed[None], scores, MASKED)
        attn_prob = low(jax.nn.softmax(scores, axis=-1))
        return jnp.einsum('hqk,kd->qhd', attn_prob, value_in, precision=lax.Precision.HIGHEST)
    attended = lax.map(jax.checkpoint(one_block), (query_in.reshape(blocks, KEY_BLOCK, HQ, HD), doc_start.reshape(blocks, KEY_BLOCK), jnp.arange(blocks, dtype=jnp.int32) * KEY_BLOCK))
    return attended.reshape(TOKENS, HQ * HD)

def reference(layer_input, lengths, gain_attn, query_down, gain_latent, query_up, key_weight, value_weight, out_weight, gain_mlp, gate_weight, up_weight, down_weight, cotangent):
    token_place = jnp.arange(TOKENS, dtype=jnp.int32)
    doc_start, position = doc_layout(lengths, token_place)
    cosine, sine = rope_tables(position, HD)

    def forward(input_f, attn_gain, down_query, latent_gain, up_query, key_proj, value_proj, out_proj, mlp_gain, gate_proj, up_proj, down_proj):
        attn_in = low(norm_rows(input_f, attn_gain))
        latent_raw = low_back(matmul(attn_in, down_query))
        latent_in = low(norm_rows(latent_raw, latent_gain))
        query_raw = low_back(matmul(latent_in, up_query)).reshape(TOKENS, HQ, HD)
        query_in = low(rotate(query_raw, cosine[:, None, :], sine[:, None, :]))
        key_in = low(rotate(low_back(matmul(attn_in, key_proj)), cosine, sine))
        value_in = low(low_back(matmul(attn_in, value_proj)))
        attended = attend(query_in, key_in, value_in, doc_start)
        attended_low = low(low_back(attended))
        hidden_in = input_f + low_back(matmul(attended_low, out_proj))
        mlp_in = low(norm_rows(hidden_in, mlp_gain))
        gate_val = low_back(matmul(mlp_in, gate_proj))
        up_val = low_back(matmul(mlp_in, up_proj))
        inner_act = low(jax.nn.silu(gate_val) * up_val)
        return hidden_in + matmul(inner_act, down_proj)
    float_args = (layer_input.astype(jnp.float32), gain_attn.astype(jnp.float32), query_down.astype(jnp.float32), gain_latent.astype(jnp.float32), query_up.astype(jnp.float32), key_weight.astype(jnp.float32), value_weight.astype(jnp.float32), out_weight.astype(jnp.float32), gain_mlp.astype(jnp.float32), gate_weight.astype(jnp.float32), up_weight.astype(jnp.float32), down_weight.astype(jnp.float32))
    output, pullback = jax.vjp(forward, *float_args)
    gradients = pullback(cotangent.astype(jnp.float32))
    return (output, gradients[0], gradients[1], gradients[2], gradients[3], gradients[4], gradients[5], gradients[6], gradients[7], gradients[8], gradients[9], gradients[10], gradients[11])
```

```python
import functools

import jax
import jax.numpy as jnp
from jax import lax
from jax.experimental import pallas as pl
from jax.experimental.pallas import tpu as pltpu
from jax.sharding import PartitionSpec as P

EPSILON = 1e-05
THETA = 10000.0
MASKED = -1000000000.0


def norm_rows(values, gain_vec):
    inverse = lax.rsqrt(jnp.mean(values * values, axis=-1, keepdims=True) + EPSILON)
    return (values * inverse * gain_vec, inverse)


def norm_back(values, inverse, gain_vec, grad_out):
    scaled = grad_out * gain_vec
    inner_dot = jnp.mean(scaled * values, axis=-1, keepdims=True)
    grad_in = scaled * inverse - values * inverse * inverse * inverse * inner_dot
    grad_gain = jnp.sum(grad_out * values * inverse, axis=0)
    return (grad_in, grad_gain)


def doc_layout(lengths, token_place):
    doc_ends = jnp.cumsum(lengths)
    doc_starts = doc_ends - lengths
    segment = jnp.sum((doc_ends[None, :] <= token_place[:, None]).astype(jnp.int32), axis=1)
    doc_index = jnp.arange(lengths.shape[0], dtype=jnp.int32)
    doc_start = jnp.sum(
        jnp.where(doc_index[None, :] == segment[:, None], doc_starts[None, :], 0), axis=1
    )
    return (doc_start, token_place - doc_start)


def rope_tables(position, head_width):
    half_width = head_width // 2
    frequency = THETA ** (-(jnp.arange(half_width, dtype=jnp.float32) * 2.0 / head_width))
    angles = position.astype(jnp.float32)[:, None] * frequency[None, :]
    return (jnp.cos(angles), jnp.sin(angles))


def rotate(values, cosine, sine):
    half_width = values.shape[-1] // 2
    front_half = values[..., :half_width]
    back_half = values[..., half_width:]
    return jnp.concatenate(
        [front_half * cosine - back_half * sine, front_half * sine + back_half * cosine], axis=-1
    )


def unrotate(values, cosine, sine):
    half_width = values.shape[-1] // 2
    front_half = values[..., :half_width]
    back_half = values[..., half_width:]
    return jnp.concatenate(
        [front_half * cosine + back_half * sine, back_half * cosine - front_half * sine], axis=-1
    )


QUERY_ROWS = 256
KEY_ROWS = 512
LOG2E = 1.4426950408889634
NT = (((1,), (1,)), ((), ()))
NN = (((1,), (0,)), ((), ()))


def dot_f32(left, right, dims):
    return lax.dot_general(left, right, dims, preferred_element_type=jnp.float32)


def tile_mask(block, base, start_row, lanes):
    key_at = block * KEY_ROWS + lax.broadcasted_iota(jnp.int32, (KEY_ROWS, lanes), 0)
    query_at = base + lax.rem(
        lax.broadcasted_iota(jnp.int32, (1, lanes), 1), jnp.int32(QUERY_ROWS)
    )
    return (key_at >= start_row) & (key_at <= query_at)


def three_loops(bounds, i, body, carry):
    carry = lax.fori_loop(bounds[i, 0], bounds[i, 1], body(True), carry)
    carry = lax.fori_loop(bounds[i, 1], bounds[i, 2], body(False), carry)
    return lax.fori_loop(bounds[i, 2], bounds[i, 3], body(True), carry)


def attend_kernel(
    heads, scale, bounds, q_ref, start_ref, k_ref, vt_ref, out_ref, lse_ref, q_all, acc
):
    i = pl.program_id(0)
    base = bounds[i, 4]
    head_dim = k_ref.shape[1]
    lanes = heads * QUERY_ROWS
    for h in range(heads):
        q_all[pl.ds(h * QUERY_ROWS, QUERY_ROWS), :] = q_ref[:, h * head_dim : (h + 1) * head_dim]
    acc[...] = jnp.zeros_like(acc)
    start_row = jnp.concatenate([start_ref[0]] * heads, axis=1)

    def body(masked):
        def step(j, carry):
            top, total = carry
            at = pl.ds(pl.multiple_of(j * KEY_ROWS, KEY_ROWS), KEY_ROWS)
            scores = dot_f32(k_ref[at, :], q_all[...], NT) * (scale * LOG2E)
            if masked:
                scores = jnp.where(tile_mask(j, base, start_row, lanes), scores, MASKED)
            new_top = jnp.maximum(top, jnp.max(scores, axis=0, keepdims=True))
            prob = jnp.exp2(scores - new_top)
            fade = jnp.exp2(top - new_top)
            total = total * fade + jnp.sum(prob, axis=0, keepdims=True)
            acc[...] = acc[...] * fade + dot_f32(vt_ref[:, at], prob.astype(jnp.bfloat16), NN)
            return new_top, total

        return step

    top, total = three_loops(
        bounds,
        i,
        body,
        (jnp.full((1, lanes), MASKED, jnp.float32), jnp.zeros((1, lanes), jnp.float32)),
    )
    lse_ref[0] = top + jnp.log2(total)
    done = acc[...] * (1.0 / total)
    for h in range(heads):
        out_ref[:, h * head_dim : (h + 1) * head_dim] = done[
            :, h * QUERY_ROWS : (h + 1) * QUERY_ROWS
        ].T.astype(jnp.bfloat16)


def attend_back_kernel(
    heads, scale, bounds, q_ref, do_ref, lse_ref, delta_ref, start_ref, cos_ref, sin_ref,
    k_ref, v_ref, kt_ref, dq_ref, dkv_ref, q_all, do_all, dqt, dk_acc, dv_acc,
):
    i = pl.program_id(0)
    base = bounds[i, 4]
    head_dim = k_ref.shape[1]
    half = head_dim // 2
    lanes = heads * QUERY_ROWS

    @pl.when(i == 0)
    def _():
        dk_acc[...] = jnp.zeros_like(dk_acc)
        dv_acc[...] = jnp.zeros_like(dv_acc)

    for h in range(heads):
        rows = pl.ds(h * QUERY_ROWS, QUERY_ROWS)
        q_all[rows, :] = q_ref[:, h * head_dim : (h + 1) * head_dim]
        do_all[rows, :] = do_ref[:, h * head_dim : (h + 1) * head_dim]
    dqt[...] = jnp.zeros_like(dqt)
    start_row = jnp.concatenate([start_ref[0]] * heads, axis=1)
    lse = lse_ref[0]
    delta = delta_ref[0]

    def body(masked):
        def step(j, carry):
            at = pl.ds(pl.multiple_of(j * KEY_ROWS, KEY_ROWS), KEY_ROWS)
            scores = dot_f32(k_ref[at, :], q_all[...], NT) * (scale * LOG2E)
            prob = jnp.exp2(scores - lse)
            if masked:
                prob = jnp.where(tile_mask(j, base, start_row, lanes), prob, 0.0)
            prob_grad = dot_f32(v_ref[at, :], do_all[...], NT)
            score_grad = (prob * (prob_grad - delta)).astype(jnp.bfloat16)
            dv_acc[at, :] += dot_f32(prob.astype(jnp.bfloat16), do_all[...], NN)
            dk_acc[at, :] += dot_f32(score_grad, q_all[...], NN)
            dqt[...] += dot_f32(kt_ref[:, at], score_grad, NN)
            return carry

        return step

    three_loops(bounds, i, body, 0)
    cosine, sine = cos_ref[...], sin_ref[...]
    for h in range(heads):
        grad = dqt[:, h * QUERY_ROWS : (h + 1) * QUERY_ROWS].T * scale
        front, back = grad[:, :half], grad[:, half:]
        dq_ref[:, h * head_dim : h * head_dim + half] = (
            front * cosine + back * sine
        ).astype(jnp.bfloat16)
        dq_ref[:, h * head_dim + half : (h + 1) * head_dim] = (
            back * cosine - front * sine
        ).astype(jnp.bfloat16)

    @pl.when(i == pl.num_programs(0) - 1)
    def _():
        dkv_ref[:, :head_dim] = (dk_acc[...] * scale).astype(jnp.bfloat16)
        dkv_ref[:, head_dim:] = dv_acc[...].astype(jnp.bfloat16)


VMEM_LIMIT = 60 * 1024 * 1024


def resident(shape):
    return pl.BlockSpec(
        shape, lambda i, bounds: tuple(0 for _ in shape), pipeline_mode=pl.Buffered(1)
    )


def row_block(width):
    return pl.BlockSpec((QUERY_ROWS, width), lambda i, bounds: (i, 0))


def lane_block(lanes):
    return pl.BlockSpec((1, 1, lanes), lambda i, bounds: (i, 0, 0))


def attend(bounds, query_in, start_rows, keys, values_t, heads):
    rows, width = query_in.shape
    window, head_dim = keys.shape
    blocks = rows // QUERY_ROWS
    lanes = heads * QUERY_ROWS
    return pl.pallas_call(
        lambda *refs: attend_kernel(heads, head_dim ** (-0.5), *refs),
        grid_spec=pltpu.PrefetchScalarGridSpec(
            num_scalar_prefetch=1,
            grid=(blocks,),
            in_specs=[
                row_block(width),
                lane_block(QUERY_ROWS),
                resident((window, head_dim)),
                resident((head_dim, window)),
            ],
            out_specs=[row_block(width), lane_block(lanes)],
            scratch_shapes=[
                pltpu.VMEM((lanes, head_dim), jnp.bfloat16),
                pltpu.VMEM((head_dim, lanes), jnp.float32),
            ],
        ),
        out_shape=[
            jax.ShapeDtypeStruct((rows, width), jnp.bfloat16),
            jax.ShapeDtypeStruct((blocks, 1, lanes), jnp.float32),
        ],
        name="attend",
        compiler_params=pltpu.CompilerParams(vmem_limit_bytes=VMEM_LIMIT),
        cost_estimate=pl.CostEstimate(
            flops=2 * 2 * rows * width * window // 2,
            bytes_accessed=4 * window * head_dim + 4 * rows * width,
            transcendentals=rows * heads * window // 2,
        ),
    )(bounds, query_in, start_rows, keys, values_t)


def attend_back(
    bounds, query_in, out_grad, lse, delta, start_rows, cosine, sine, keys, values, keys_t, heads
):
    rows, width = query_in.shape
    window, head_dim = keys.shape
    blocks = rows // QUERY_ROWS
    lanes = heads * QUERY_ROWS
    return pl.pallas_call(
        lambda *refs: attend_back_kernel(heads, head_dim ** (-0.5), *refs),
        grid_spec=pltpu.PrefetchScalarGridSpec(
            num_scalar_prefetch=1,
            grid=(blocks,),
            in_specs=[
                row_block(width),
                row_block(width),
                lane_block(lanes),
                lane_block(lanes),
                lane_block(QUERY_ROWS),
                row_block(head_dim // 2),
                row_block(head_dim // 2),
                resident((window, head_dim)),
                resident((window, head_dim)),
                resident((head_dim, window)),
            ],
            out_specs=[
                row_block(width),
                resident((window, 2 * head_dim)),
            ],
            scratch_shapes=[
                pltpu.VMEM((lanes, head_dim), jnp.bfloat16),
                pltpu.VMEM((lanes, head_dim), jnp.bfloat16),
                pltpu.VMEM((head_dim, lanes), jnp.float32),
                pltpu.VMEM((window, head_dim), jnp.float32),
                pltpu.VMEM((window, head_dim), jnp.float32),
            ],
        ),
        out_shape=[
            jax.ShapeDtypeStruct((rows, width), jnp.bfloat16),
            jax.ShapeDtypeStruct((window, 2 * head_dim), jnp.bfloat16),
        ],
        name="attend_back",
        compiler_params=pltpu.CompilerParams(vmem_limit_bytes=VMEM_LIMIT),
        cost_estimate=pl.CostEstimate(
            flops=5 * 2 * rows * width * window // 2,
            bytes_accessed=6 * window * head_dim + 8 * rows * width,
            transcendentals=rows * heads * window // 2,
        ),
    )(bounds, query_in, out_grad, lse, delta, start_rows, cosine, sine, keys, values, keys_t)


MESH = pl.DeviceIdType.MESH


def line_kernel(n, chunks, step, add, *refs):
    if add:
        part, extra, full, from_left, from_right, sends, send_s, recv_s, gsend_s, grecv_s = refs
    else:
        part, full, from_left, from_right, sends, send_s, recv_s, gsend_s, grecv_s = refs
    me = lax.axis_index("tp")
    has_left, has_right = me > 0, me < n - 1
    left, right = jnp.maximum(me - 1, 0), jnp.minimum(me + 1, n - 1)

    def to(side):
        return {"tp": right if side == 0 else left}

    def neighbour(side):
        return has_right if side == 0 else has_left

    barrier = pltpu.get_barrier_semaphore()
    for side in range(2):
        @pl.when(neighbour(side))
        def _(side=side):
            pl.semaphore_signal(barrier, inc=1, device_id=to(side), device_id_type=MESH)
    pl.semaphore_wait(barrier, has_left.astype(jnp.int32) + has_right.astype(jnp.int32))

    def came(side):
        return has_left if side == 0 else has_right

    inbox = (from_left, from_right)

    def reduce_copy(side, c, d, src):
        return pltpu.make_async_remote_copy(
            src_ref=src, dst_ref=inbox[side].at[c, d],
            send_sem=send_s.at[side, c, d], recv_sem=recv_s.at[side, c, d],
            device_id=to(side), device_id_type=MESH)

    def gather_copy(side, c, j):
        return pltpu.make_async_remote_copy(
            src_ref=full.at[c, j], dst_ref=full.at[c, j],
            send_sem=gsend_s.at[side, c, j], recv_sem=grecv_s.at[side, c, j],
            device_id=to(side), device_id_type=MESH)

    def reduce_side(side, c):
        for k in range(n - 1):
            d = n - 1 - k if side == 0 else k
            ahead = (me < d) if side == 0 else (me > d)
            @pl.when(ahead & came(side))
            def _(d=d):
                reduce_copy(side, c, d, inbox[side].at[c, d]).wait_recv()
                total = part[c, d].astype(jnp.float32) + inbox[side][c, d].astype(jnp.float32)
                sends[c, d] = total.astype(jnp.bfloat16)
                reduce_copy(side, c, d, sends.at[c, d]).start()
            @pl.when(ahead & jnp.logical_not(came(side)))
            def _(d=d):
                reduce_copy(side, c, d, part.at[c, d]).start()

    def finish_step(c):
        for side in range(2):
            @pl.when(came(side))
            def _(side=side):
                reduce_copy(side, c, me, inbox[side].at[c, me]).wait_recv()
        total = part[c, me].astype(jnp.float32)
        if add:
            total += extra[c, me].astype(jnp.float32)
        got = jnp.where(has_left, from_left[c, me].astype(jnp.float32), 0.0)
        got += jnp.where(has_right, from_right[c, me].astype(jnp.float32), 0.0)
        full[c, me] = (total + got).astype(jnp.bfloat16)
        for side in range(2):
            @pl.when(neighbour(side))
            def _(side=side):
                gather_copy(side, c, me).start()

    def within(c):
        return (c >= 0) & (c < chunks)

    def settled(j):
        return step * jnp.maximum(j, n - 1 - j)

    last = chunks + step * 2 * (n - 1)

    @pl.loop(0, last)
    def _(t):
        for side in range(2):
            c = t - step * (me if side == 0 else n - 1 - me)
            @pl.when(within(c))
            def _(side=side, c=c):
                reduce_side(side, c)
        c_end = t - settled(me)
        @pl.when(within(c_end))
        def _():
            finish_step(c_end)
        for k in range(1, n):
            for side in range(2):
                j = me - k if side == 0 else me + k
                c = t - settled(j) - step * k
                there = (j >= 0) if side == 0 else (j < n)
                @pl.when(there & within(c))
                def _(side=side, j=j, c=c):
                    gather_copy(side, c, j).wait_recv()
                    @pl.when(neighbour(side))
                    def _():
                        gather_copy(side, c, j).start()

    @pl.loop(0, chunks)
    def _(c):
        for d in range(n):
            for side in range(2):
                ahead = (me < d) if side == 0 else (me > d)
                @pl.when(ahead)
                def _(side=side, d=d):
                    reduce_copy(side, c, d, sends.at[c, d]).wait_send()
                sent = ((d <= me) if side == 0 else (d >= me)) & neighbour(side)
                @pl.when(sent)
                def _(side=side, d=d):
                    gather_copy(side, c, d).wait_send()

def line_all_reduce(part, extra, n, cid, step=1):
    rows, width = part.shape
    chunks = rows // (16 * n)
    shape = (chunks, n, rows // (chunks * n), width)
    args = [part.reshape(shape)] + ([] if extra is None else [extra.reshape(shape)])
    V = pl.BlockSpec(memory_space=pltpu.VMEM)
    out = pl.pallas_call(
        functools.partial(line_kernel, n, chunks, step, extra is not None),
        out_shape=jax.ShapeDtypeStruct(shape, jnp.bfloat16),
        in_specs=[V] * len(args), out_specs=V,
        scratch_shapes=[pltpu.VMEM(shape, jnp.bfloat16)] * 3 + [pltpu.SemaphoreType.DMA((2, chunks, n))] * 4,
        name="line_all_reduce",
        compiler_params=pltpu.CompilerParams(collective_id=cid, has_side_effects=True, vmem_limit_bytes=VMEM_LIMIT),
        cost_estimate=pl.CostEstimate(flops=rows * width, bytes_accessed=100 * rows * width, transcendentals=0),
    )(*args)
    return out.reshape(rows, width)


def chain_kernel(ranks, reach, chunks, part, total, inbox, sends, send_s, recv_s):
    me = lax.axis_index("seq")
    receives, gives = me < ranks - 1, me > 0
    target = {"seq": jnp.maximum(me - 1, 0)}
    barrier = pltpu.get_barrier_semaphore()

    @pl.when(receives)
    def _():
        pl.semaphore_signal(
            barrier, inc=1, device_id={"seq": jnp.minimum(me + 1, ranks - 1)}, device_id_type=MESH
        )

    @pl.when(gives)
    def _():
        pl.semaphore_wait(barrier, 1)

    def hop(w, c, src):
        return pltpu.make_async_remote_copy(
            src_ref=src,
            dst_ref=inbox.at[w, c],
            send_sem=send_s.at[w, c],
            recv_sem=recv_s.at[w, c],
            device_id=target,
            device_id_type=MESH,
        )

    @pl.loop(0, chunks + reach)
    def _(t):
        for w in range(reach + 1):
            c = t - w
            live = (c >= 0) & (c < chunks) & (me - reach + w >= 0)
            if w == 0:

                @pl.when(live & gives)
                def _(c=c):
                    hop(0, c, part.at[0, c]).start()

            elif w < reach:

                @pl.when(live & receives & gives)
                def _(w=w, c=c):
                    hop(w - 1, c, part.at[w, c]).wait_recv()
                    sends[w, c] = (
                        part[w, c].astype(jnp.float32) + inbox[w - 1, c].astype(jnp.float32)
                    ).astype(jnp.bfloat16)
                    hop(w, c, sends.at[w, c]).start()

                @pl.when(live & jnp.logical_not(receives) & gives)
                def _(w=w, c=c):
                    hop(w, c, part.at[w, c]).start()

            else:

                @pl.when(live & receives)
                def _(c=c):
                    hop(reach - 1, c, part.at[reach, c]).wait_recv()
                    total[c] = (
                        part[reach, c].astype(jnp.float32)
                        + inbox[reach - 1, c].astype(jnp.float32)
                    ).astype(jnp.bfloat16)

                @pl.when(live & jnp.logical_not(receives))
                def _(c=c):
                    total[c] = part[reach, c]

    @pl.loop(0, chunks)
    def _(c):
        for w in range(reach):

            @pl.when((me - reach + w >= 0) & gives)
            def _(w=w):
                hop(w, c, part.at[w, c]).wait_send()


def chain_reduce(part, ranks, rows, cid, chunks=8):
    window, width = part.shape
    reach = window // rows - 1
    shape = (reach + 1, chunks, rows // chunks, width)
    V = pl.BlockSpec(memory_space=pltpu.VMEM)
    out = pl.pallas_call(
        functools.partial(chain_kernel, ranks, reach, chunks),
        out_shape=jax.ShapeDtypeStruct(shape[1:], jnp.bfloat16),
        in_specs=[V],
        out_specs=V,
        scratch_shapes=[pltpu.VMEM((reach,) + shape[1:], jnp.bfloat16)] * 2
        + [pltpu.SemaphoreType.DMA((reach, chunks))] * 2,
        name="chain_reduce",
        compiler_params=pltpu.CompilerParams(
            collective_id=cid, has_side_effects=True, vmem_limit_bytes=VMEM_LIMIT
        ),
        cost_estimate=pl.CostEstimate(
            flops=rows * width, bytes_accessed=100 * rows * width, transcendentals=0
        ),
    )(part.reshape(shape))
    return out.reshape(rows, width)


def on_device(
    layer_input,
    lengths,
    gain_attn,
    query_down,
    gain_latent,
    query_up,
    key_weight,
    value_weight,
    out_weight,
    gain_mlp,
    gate_weight,
    up_weight,
    down_weight,
    cotangent,
):
    rows_here = layer_input.shape[0]
    own_cols = layer_input.shape[1]
    seq_rank = lax.axis_index("seq")
    tp_rank = lax.axis_index("tp")
    tp_count = lax.axis_size("tp")
    all_tokens = rows_here * lax.axis_size("seq")
    head_dim = key_weight.shape[1]
    local_heads = query_up.shape[1] // head_dim
    latent = query_down.shape[1]
    col_start = tp_rank * own_cols
    whole_x = lax.all_gather(layer_input, "tp", axis=1, tiled=True)
    input_f = whole_x.astype(jnp.float32)
    attn_gain = gain_attn.astype(jnp.float32)
    normed_one, inverse_one = norm_rows(input_f, attn_gain)
    attn_in = normed_one.astype(jnp.bfloat16)
    latent_raw = jnp.dot(attn_in, query_down, preferred_element_type=jnp.float32)
    latent_gain = gain_latent.astype(jnp.float32)
    latent_norm, inverse_lat = norm_rows(latent_raw, latent_gain)
    latent_in = latent_norm.astype(jnp.bfloat16)
    token_place = seq_rank * rows_here + jnp.arange(rows_here, dtype=jnp.int32)
    doc_start, position = doc_layout(lengths, token_place)
    cosine, sine = rope_tables(position, head_dim)
    query_raw = jnp.dot(latent_in, query_up, preferred_element_type=jnp.float32).reshape(
        rows_here, local_heads, head_dim
    )
    query_in = (
        rotate(query_raw, cosine[:, None, :], sine[:, None, :])
        .astype(jnp.bfloat16)
        .reshape(rows_here, local_heads * head_dim)
    )
    key_mine = rotate(
        jnp.dot(attn_in, key_weight, preferred_element_type=jnp.float32), cosine, sine
    ).astype(jnp.bfloat16)
    value_mine = jnp.dot(attn_in, value_weight, preferred_element_type=jnp.float32).astype(
        jnp.bfloat16
    )
    both_mine = jnp.concatenate([key_mine, value_mine], axis=1)
    both_all = lax.all_gather(both_mine, "seq", axis=0, tiled=True)
    cotangent, _ = lax.optimization_barrier((cotangent, both_all))
    grad_rows = lax.all_gather(cotangent, "tp", axis=1, tiled=True)
    window = all_tokens // 2 + rows_here
    window_start = (seq_rank + 1) * rows_here - window
    both_padded = jnp.concatenate(
        [jnp.zeros((window - rows_here, 2 * head_dim), jnp.bfloat16), both_all], axis=0
    )
    both_win = lax.dynamic_slice_in_dim(both_padded, seq_rank * rows_here, window, 0)
    keys_win, values_win = both_win[:, :head_dim], both_win[:, head_dim:]
    blocks = rows_here // QUERY_ROWS
    start_rows = (doc_start - window_start).reshape(blocks, 1, QUERY_ROWS)
    block_base = (
        seq_rank * rows_here - window_start + jnp.arange(blocks, dtype=jnp.int32) * QUERY_ROWS
    )
    low_key, high_key = start_rows[:, 0, 0], start_rows[:, 0, QUERY_ROWS - 1]
    last_tile = (block_base + QUERY_ROWS + KEY_ROWS - 1) // KEY_ROWS
    full_from = jnp.minimum((high_key + KEY_ROWS - 1) // KEY_ROWS, last_tile)
    full_to = jnp.maximum(full_from, (block_base + 1) // KEY_ROWS)
    bounds = jnp.stack(
        [low_key // KEY_ROWS, full_from, full_to, last_tile, block_base], axis=1
    ).astype(jnp.int32)
    attended_low, log_total = attend(
        bounds, query_in, start_rows, keys_win, values_win.T, local_heads
    )
    proj_part = jnp.dot(attended_low, out_weight, preferred_element_type=jnp.float32)
    hidden_low = line_all_reduce(proj_part.astype(jnp.bfloat16), whole_x, tp_count, 1)
    hidden_in = hidden_low.astype(jnp.float32)
    resid_mine = lax.dynamic_slice_in_dim(hidden_in, col_start, own_cols, 1)
    mlp_gain = gain_mlp.astype(jnp.float32)
    normed_two, inverse_two = norm_rows(hidden_in, mlp_gain)
    mlp_in = normed_two.astype(jnp.bfloat16)
    gate_val = jnp.dot(mlp_in, gate_weight, preferred_element_type=jnp.float32)
    up_val = jnp.dot(mlp_in, up_weight, preferred_element_type=jnp.float32)
    gate_sig = jax.nn.sigmoid(gate_val)
    gate_act = gate_val * gate_sig
    inner_act = (gate_act * up_val).astype(jnp.bfloat16)
    down_part = jnp.dot(inner_act, down_weight, preferred_element_type=jnp.float32)
    down_mine = lax.psum_scatter(
        down_part.astype(jnp.bfloat16), "tp", scatter_dimension=1, tiled=True
    ).astype(jnp.float32)
    layer_output = resid_mine + down_mine
    inner_grad = jnp.einsum("td,fd->tf", grad_rows, down_weight, preferred_element_type=jnp.float32)
    gate_grad = (inner_grad * up_val * gate_sig * (1.0 + gate_val * (1.0 - gate_sig))).astype(
        jnp.bfloat16
    )
    up_grad = (inner_grad * gate_act).astype(jnp.bfloat16)
    down_weight_grad = jnp.einsum(
        "tf,td->fd", inner_act, grad_rows, preferred_element_type=jnp.float32
    )
    gate_weight_grad = jnp.einsum(
        "td,tf->df", mlp_in, gate_grad, preferred_element_type=jnp.float32
    )
    up_weight_grad = jnp.einsum("td,tf->df", mlp_in, up_grad, preferred_element_type=jnp.float32)
    mlp_part = jnp.einsum(
        "tf,df->td", gate_grad, gate_weight, preferred_element_type=jnp.float32
    ) + jnp.einsum("tf,df->td", up_grad, up_weight, preferred_element_type=jnp.float32)
    mlp_low = line_all_reduce(mlp_part.astype(jnp.bfloat16), None, tp_count, 2)
    mlp_back = mlp_low.astype(jnp.float32)
    norm_two_grad, gain_mlp_grad = norm_back(hidden_in, inverse_two, mlp_gain, mlp_back)
    hidden_grad = grad_rows.astype(jnp.float32) + norm_two_grad
    branch_grad = hidden_grad.astype(jnp.bfloat16)
    out_weight_grad = jnp.einsum(
        "tc,td->cd", attended_low, branch_grad, preferred_element_type=jnp.float32
    )
    attended_grad = jnp.einsum(
        "td,cd->tc", branch_grad, out_weight, preferred_element_type=jnp.float32
    ).astype(jnp.bfloat16)
    row_delta = jnp.sum(
        (attended_grad.astype(jnp.float32) * attended_low.astype(jnp.float32)).reshape(
            blocks, QUERY_ROWS, local_heads, head_dim
        ),
        axis=-1,
    )
    delta_rows = jnp.swapaxes(row_delta, 1, 2).reshape(blocks, 1, local_heads * QUERY_ROWS)
    query_back, both_win_grad = attend_back(
        bounds,
        query_in,
        attended_grad,
        log_total,
        delta_rows,
        start_rows,
        cosine,
        sine,
        keys_win,
        values_win,
        keys_win.T,
        local_heads,
    )
    both_sum = chain_reduce(both_win_grad, lax.axis_size("seq"), rows_here, 3)
    query_up_grad = jnp.einsum(
        "tr,tc->rc", latent_in, query_back, preferred_element_type=jnp.float32
    )
    latent_part = jnp.einsum("tc,rc->tr", query_back, query_up, preferred_element_type=jnp.float32)
    back_low = line_all_reduce(
        jnp.concatenate([latent_part.astype(jnp.bfloat16), both_sum], axis=1), None, tp_count, 4
    )
    back_all = back_low.astype(jnp.float32)
    latent_back = back_all[:, :latent]
    key_total = back_all[:, latent : latent + head_dim]
    value_total = back_all[:, latent + head_dim :]
    key_back = unrotate(key_total, cosine, sine).astype(jnp.bfloat16)
    value_back = value_total.astype(jnp.bfloat16)
    latent_grad_in, gain_latent_grad = norm_back(latent_raw, inverse_lat, latent_gain, latent_back)
    latent_low = latent_grad_in.astype(jnp.bfloat16)
    lat_width = latent // tp_count
    lat_slice = lax.dynamic_slice_in_dim(latent_low, tp_rank * lat_width, lat_width, 1)
    query_down_grad = jnp.einsum(
        "td,tr->dr", attn_in, lat_slice, preferred_element_type=jnp.float32
    )
    attn_in_cols = lax.dynamic_slice_in_dim(attn_in, col_start, own_cols, 1)
    key_weight_grad = jnp.einsum(
        "td,tk->dk", attn_in_cols, key_back, preferred_element_type=jnp.float32
    )
    value_weight_grad = jnp.einsum(
        "td,tk->dk", attn_in_cols, value_back, preferred_element_type=jnp.float32
    )
    down_cols = lax.dynamic_slice_in_dim(query_down, col_start, own_cols, 0)
    key_cols = lax.dynamic_slice_in_dim(key_weight, col_start, own_cols, 0)
    value_cols = lax.dynamic_slice_in_dim(value_weight, col_start, own_cols, 0)
    first_back = (
        jnp.einsum("tr,dr->td", latent_low, down_cols, preferred_element_type=jnp.float32)
        + jnp.einsum("tk,dk->td", key_back, key_cols, preferred_element_type=jnp.float32)
        + jnp.einsum("tk,dk->td", value_back, value_cols, preferred_element_type=jnp.float32)
    )
    row_dot = (
        jnp.sum(latent_low.astype(jnp.float32) * latent_raw, axis=-1, keepdims=True)
        + jnp.sum(key_total * key_mine.astype(jnp.float32), axis=-1, keepdims=True)
        + jnp.sum(value_total * value_mine.astype(jnp.float32), axis=-1, keepdims=True)
    )
    x_mine = layer_input.astype(jnp.float32)
    gain_mine = lax.dynamic_slice_in_dim(attn_gain, col_start, own_cols, 0)
    norm_one_grad = inverse_one * (
        first_back * gain_mine - x_mine * inverse_one * (row_dot / input_f.shape[1])
    )
    gain_attn_mine = jnp.sum(first_back * x_mine * inverse_one, axis=0)
    hidden_grad_mine = lax.dynamic_slice_in_dim(hidden_grad, col_start, own_cols, 1)
    input_grad = hidden_grad_mine + norm_one_grad

    def own_place(mine, full):
        return lax.dynamic_update_slice_in_dim(jnp.zeros((full,), jnp.bfloat16), mine, col_start, 0)

    gains = jnp.concatenate(
        [
            own_place(gain_attn_mine.astype(jnp.bfloat16), input_f.shape[1]),
            own_place(
                lax.dynamic_slice_in_dim(gain_mlp_grad, col_start, own_cols, 0).astype(jnp.bfloat16),
                input_f.shape[1],
            ),
            jnp.where(tp_rank == 0, gain_latent_grad, 0.0).astype(jnp.bfloat16),
        ]
    )
    gains = lax.psum(gains, ("seq", "tp")).astype(jnp.float32)
    model = input_f.shape[1]
    gain_attn_grad, gain_mlp_grad, gain_latent_grad = (
        gains[:model],
        gains[model : 2 * model],
        gains[2 * model :],
    )

    def low(value):
        return value.astype(jnp.bfloat16)

    def after(values, done):
        return lax.optimization_barrier((values, done))[0]

    down_sum = lax.psum(low(down_weight_grad), "seq")
    pair = after((low(gate_weight_grad), low(up_weight_grad)), down_sum)
    gate_sum, up_sum = lax.psum(pair, "seq")
    out_sum = lax.psum(after(low(out_weight_grad), (gate_sum, up_sum)), "seq")
    tail = (
        low(query_down_grad),
        low(query_up_grad),
        low(key_weight_grad),
        low(value_weight_grad),
    )
    tail = lax.psum(after(tail, out_sum), "seq")
    query_down_grad, query_up_grad, key_weight_grad, value_weight_grad = [
        value.astype(jnp.float32) for value in tail
    ]
    out_weight_grad = out_sum.astype(jnp.float32)
    down_weight_grad = down_sum.astype(jnp.float32)
    gate_weight_grad = gate_sum.astype(jnp.float32)
    up_weight_grad = up_sum.astype(jnp.float32)
    return (
        layer_output,
        input_grad,
        gain_attn_grad,
        query_down_grad,
        gain_latent_grad,
        query_up_grad,
        key_weight_grad,
        value_weight_grad,
        out_weight_grad,
        gain_mlp_grad,
        gate_weight_grad,
        up_weight_grad,
        down_weight_grad,
    )


def solution(mesh):
    in_specs = (
        P("seq", "tp"),
        P(),
        P(),
        P(),
        P(),
        P(None, "tp"),
        P(),
        P(),
        P("tp", None),
        P(),
        P(None, "tp"),
        P(None, "tp"),
        P("tp", None),
        P("seq", "tp"),
    )
    out_specs = (
        P("seq", "tp"),
        P("seq", "tp"),
        P(),
        P(None, "tp"),
        P(),
        P(None, "tp"),
        P("tp", None),
        P("tp", None),
        P("tp", None),
        P(),
        P(None, "tp"),
        P(None, "tp"),
        P("tp", None),
    )
    return jax.shard_map(
        on_device, mesh=mesh, in_specs=in_specs, out_specs=out_specs, check_vma=False
    )
```
